32 devices in a mesh: px: 8 (over z, y), py: 4 (over x, core).
Axes of the slice: x: 2, y: 2, z: 4, core: 2. Of those that a mesh axis runs over, the one named last changes fastest.
Arguments:
- point_channel_values: bfloat16 [4096, 64, 128], P(('px', 'py')), may hold values from -6 to 6
- point_offsets: bfloat16 [4096, 3, 128], P(('px', 'py')), may hold values from -1 to 17
- point_counts: int32 [4096], P(('px', 'py')), may hold values from 1 to 128
- block_bricks: int32 [4096, 4], P(('px', 'py')), may hold values from 0 to 16383, as said below
- spectral_weights: bfloat16 [2, 32, 32, 32, 64, 128], P(None, None, 'px', 'py'), may hold values from -0.5 to 0.5
- skip_weights: bfloat16 [2, 64, 64], replicated, may hold values from -0.75 to 0.75
- skip_bias: float32 [2, 64], replicated, may hold values from -3 to 3
Outputs:
- decoded: bfloat16 [4096, 64, 128], P(('px', 'py'))
The draws below stay inside these ranges and needn't reach their ends.
Inputs may be any that keep to these rules, and one draw needn't show every extreme that they name: `block_bricks`: the 4 bricks of a block are distinct and lie on one device. Among the 128 blocks of one device at most 8 have their bricks on any one device, and in every draw some device receives exactly 8 blocks from every device.
All inputs are finite; a program needn't handle non-finite values.
Results may differ from the reference program's by a relative error of at most 0.0075.
Values may be sent and summed in bfloat16 or wider, within the bound.
A program may use at most 256 MiB of HBM per device.

```python
import math
import jax
import jax.numpy as jnp
from jax import lax

CH = 64
MODES = 32
NX = 128
NY = 128
NZ = 128
LAYERS = 2
BLOCK = 128
HALO = 4
BLK_DEV = 128
CAPB = 8
NBLK = 4096
BY = 8
BZ = 8
BRK_DEV = 512
N_PX = 8
N_PY = 4
DEVICES = 32


def draw_block_bricks(key, part):
    hot_key, device_key = jax.random.split(key)
    hottest = jax.random.randint(hot_key, (), 0, DEVICES)

    def per_source(source_point):
        source_key = jax.random.fold_in(device_key, source_point)
        pick_key, shuffle_key, brick_key = jax.random.split(source_key, 3)
        chosen = jax.random.permutation(pick_key, (DEVICES - 1) * CAPB)[:BLK_DEV - CAPB]
        others = chosen // CAPB
        others = others + (others >= hottest).astype(others.dtype)
        owners = jnp.concatenate([jnp.full((CAPB,), hottest, jnp.int32), others.astype(jnp.int32)])
        owners = jax.random.permutation(shuffle_key, owners)
        home_bricks = jax.random.randint(brick_key, (BLK_DEV,), 0, BRK_DEV)
        return (owners, home_bricks)
    owners, home_bricks = jax.vmap(per_source)(jnp.arange(DEVICES, dtype=jnp.int32))
    first_coord = home_bricks // (BY * BZ)
    second_coord = home_bricks // BZ % BY
    third_coord = home_bricks % BZ
    flip_first = (jnp.bitwise_xor(first_coord, 1) * BY + second_coord) * BZ + third_coord
    flip_second = (first_coord * BY + jnp.bitwise_xor(second_coord, 1)) * BZ + third_coord
    flip_third = (first_coord * BY + second_coord) * BZ + jnp.bitwise_xor(third_coord, 1)
    listed = jnp.stack([home_bricks, flip_first, flip_second, flip_third], axis=-1)
    return (owners[..., None] * BRK_DEV + listed).reshape(NBLK, HALO).astype(jnp.int32)


def draw_point_offsets(key, part):
    uniform_draw = jax.random.uniform(key, (NBLK, 3, BLOCK), jnp.float32)
    extent = jnp.array([2.0, 4.0, 16.0], jnp.float32)[None, :, None]
    return (-1.0 + uniform_draw * (extent + 2.0)).astype(jnp.bfloat16)


def touch_ends(result, stream_key, smallest, largest):
    longest = result.shape.index(max(result.shape))
    spots = []
    for shift in (0, 1):
        where = [jax.random.randint(jax.random.fold_in(stream_key, axis), (), 0, length) for axis, length in enumerate(result.shape)]
        where[longest] = (where[longest] + shift) % result.shape[longest]
        spots.append(tuple(where))
    return result.at[spots[0]].set(smallest).at[spots[1]].set(largest)


def levels(stream_key, dims, cuts, smallest, top_value):
    factor_of = 1.0
    for axis_at, shards_of in cuts:
        steps = jax.random.uniform(jax.random.fold_in(jax.random.fold_in(stream_key, 6), axis_at), (shards_of,), jnp.float32, smallest / len(cuts), top_value / len(cuts))
        factor_of = factor_of * jnp.repeat(jnp.exp(steps), dims[axis_at] // shards_of).reshape((-1,) + (1,) * (len(dims) - 1 - axis_at))
    return factor_of


def gaussian(rng, shape, scale, limit, pieces=(), kind=jnp.bfloat16):
    entries = jax.random.normal(rng, shape, jnp.float32) * scale
    if len(pieces) > 0:
        entries = levels(rng, shape, pieces, -0.22, 0.18) * entries
    return jnp.clip(entries, min=-limit, max=limit).astype(kind)


def setup_inputs(seed: int = 0) -> dict:
    key_of = jax.random.split(jax.random.key(seed), 8)
    return {
        "point_channel_values": gaussian(key_of[0], (NBLK, CH, BLOCK), 1.0, 6.0, ((0, 32),)),
        "point_offsets": draw_point_offsets(jax.random.fold_in(key_of[7], 71), 0),
        "point_counts": touch_ends(jax.random.randint(key_of[2], (NBLK,), 1, BLOCK + 1), jax.random.fold_in(key_of[2], 1), 1, BLOCK).astype(jnp.int32),
        "block_bricks": draw_block_bricks(jax.random.fold_in(key_of[7], 71), 0),
        "spectral_weights": gaussian(key_of[4], (LAYERS, MODES, MODES, MODES, CH, 2 * CH), (2 * CH) ** -0.5, 0.5, ((2, 8), (3, 4))),
        "skip_weights": gaussian(key_of[5], (LAYERS, CH, CH), CH ** -0.5, 0.75),
        "skip_bias": gaussian(key_of[6], (LAYERS, CH), 0.5, 3.0, (), jnp.float32),
    }


AMPLITUDE = 0.25
SPREAD = 4.5
DECODE_SCALE = 0.1


def cell_centers():
    cell_index = jnp.arange(128, dtype=jnp.int32)
    return jnp.stack([cell_index // 64, (cell_index // 16) % 4, cell_index % 16]).astype(jnp.float32) + 0.5


def brick_anchor(local_ids, bricks_y, bricks_z):
    clamped_weights = jnp.maximum(local_ids, 0)
    return jnp.stack([2 * (clamped_weights // (bricks_y * bricks_z)), 4 * ((clamped_weights // bricks_z) % bricks_y), 16 * (clamped_weights % bricks_z)], axis=-1).astype(jnp.float32)


def block_work(features, offsets, counts, local_ids, bricks_y, bricks_z):
    total_items, channels, points = features.shape
    group_size = math.gcd(total_items, 16)
    centers = cell_centers()

    def one_group(items):
        feature_share, offset_part, count_part, id_part = items
        validity = (jnp.arange(points, dtype=jnp.int32)[None, :] < count_part[:, None]).astype(jnp.float32)
        anchors = brick_anchor(id_part, bricks_y, bricks_z)
        relative_position = anchors - anchors[:, :1, :]
        placed = offset_part.astype(jnp.float32)[:, None, :, :] - relative_position[:, :, :, None]
        apart = placed[..., None] - centers[None, None, :, None, :]
        distance = jnp.sum(apart * apart, axis=2)
        kernel_weight_value = (AMPLITUDE * jnp.exp(-distance / SPREAD) * validity[:, None, :, None]).astype(jnp.bfloat16)
        brick_tile_grid = jnp.einsum('dqw,dewn->deqn', feature_share.astype(jnp.float32), kernel_weight_value.astype(jnp.float32)).astype(jnp.bfloat16)
        return kernel_weight_value, brick_tile_grid

    grouped = tuple(member.reshape((total_items // group_size, group_size) + member.shape[1:]) for member in (features, offsets, counts, local_ids))
    kernel_weight_value, brick_tile_grid = lax.map(one_group, grouped)
    return kernel_weight_value.reshape((total_items,) + kernel_weight_value.shape[2:]), brick_tile_grid.reshape((total_items,) + brick_tile_grid.shape[2:])


def decode_points(brick_values, kernel_weight_value):
    summed = jnp.einsum('nhcx,nhpx->ncp', brick_values.astype(jnp.float32), kernel_weight_value.astype(jnp.float32))
    return (DECODE_SCALE * summed).astype(jnp.bfloat16)


def round_half(values):
    lowered = values.astype(jnp.bfloat16)
    lowered = lax.optimization_barrier(lowered)
    return lowered.astype(values.dtype)


def round_complex(values):
    return lax.complex(round_half(jnp.real(values)), round_half(jnp.imag(values)))


def keep_index(length, kept_modes):
    half_modes = kept_modes // 2
    return jnp.concatenate([jnp.arange(half_modes, dtype=jnp.int32), jnp.arange(length - half_modes, length, dtype=jnp.int32)]).astype(jnp.int32)


def spectral_reference(grid, weights):
    third_modes = round_complex(jnp.fft.rfft(grid, axis=3, norm="ortho")[..., :MODES])
    second_modes = round_complex(jnp.take(jnp.fft.fft(third_modes, axis=2, norm="ortho"), keep_index(NY, MODES), axis=2))
    first_modes = round_complex(jnp.take(jnp.fft.fft(second_modes, axis=1, norm="ortho"), keep_index(NX, MODES), axis=1))
    real_part = jnp.real(first_modes).transpose(1, 2, 3, 0)
    imag_part = jnp.imag(first_modes).transpose(1, 2, 3, 0)

    def mix_slice(items):
        left_real, left_imag, weight_slice = items
        weight_full = weight_slice.astype(real_part.dtype)
        from_real = jnp.einsum('kzc,kzcr->kzr', left_real, weight_full, precision=lax.Precision.HIGHEST)
        from_imag = jnp.einsum('kzc,kzcr->kzr', left_imag, weight_full, precision=lax.Precision.HIGHEST)
        return from_real[..., :CH] - from_imag[..., CH:], from_real[..., CH:] + from_imag[..., :CH]

    mixed_real, mixed_imag = lax.map(mix_slice, (real_part, imag_part, weights))
    mixed = lax.complex(mixed_real, mixed_imag).transpose(3, 0, 1, 2)
    widened = jnp.zeros((CH, NX, MODES, MODES), mixed.dtype).at[:, keep_index(NX, MODES)].set(mixed)
    first_back = round_complex(jnp.fft.ifft(widened, axis=1, norm="ortho"))
    widened = jnp.zeros((CH, NX, NY, MODES), first_back.dtype).at[:, :, keep_index(NY, MODES)].set(first_back)
    second_back = round_complex(jnp.fft.ifft(widened, axis=2, norm="ortho"))
    return jnp.fft.irfft(second_back, n=NZ, axis=3, norm="ortho")


def global_grid(bricks, bricks_along_first, bricks_y, bricks_z):
    shaped = bricks.reshape(N_PX, N_PY, bricks_along_first, bricks_y, bricks_z, CH, 2, 4, 16)
    return shaped.transpose(5, 0, 2, 6, 1, 3, 7, 4, 8).reshape(CH, NX, NY, NZ)


def global_bricks(grid, bricks_along_first, bricks_y, bricks_z):
    shaped = grid.reshape(CH, N_PX, bricks_along_first, 2, N_PY, bricks_y, 4, bricks_z, 16)
    return shaped.transpose(1, 4, 2, 5, 7, 0, 3, 6, 8).reshape(N_PX * N_PY * bricks_along_first * bricks_y * bricks_z, CH, 128)


def reference(point_channel_values, point_offsets, point_counts, block_bricks, spectral_weights, skip_weights, skip_bias):
    bricks_along_first = NX // N_PX // 2
    bricks_y = NY // N_PY // 4
    bricks_z = NZ // 16
    bricks_device = bricks_along_first * bricks_y * bricks_z
    total_bricks = bricks_device * N_PX * N_PY
    block_total = point_channel_values.shape[0]
    group_size = math.gcd(block_total, 256)
    local_ids = block_bricks % bricks_device
    stacked = tuple(member.reshape((block_total // group_size, group_size) + member.shape[1:]) for member in (point_channel_values, point_offsets, point_counts, local_ids, block_bricks))

    def add_group(brick_sums, items):
        features, offsets, counts, local_part, global_part = items
        unused, brick_tile_grid = block_work(features, offsets, counts, local_part, bricks_y, bricks_z)
        flat_tiles = brick_tile_grid.reshape((-1,) + brick_tile_grid.shape[2:]).astype(jnp.float32)
        return brick_sums.at[global_part.reshape(-1)].add(flat_tiles), None

    brick_sums, unused = lax.scan(add_group, jnp.zeros((total_bricks, CH, 128), jnp.float32), stacked)
    grid = global_grid(brick_sums.astype(jnp.bfloat16), bricks_along_first, bricks_y, bricks_z)
    for depth_index in range(LAYERS):
        spectral = spectral_reference(grid.astype(jnp.float32), spectral_weights[depth_index])
        skipped = jnp.einsum('io,ixyz->oxyz', skip_weights[depth_index].astype(jnp.float32), grid.astype(jnp.float32), precision=lax.Precision.HIGHEST)
        grid = jax.nn.gelu(spectral + skipped + skip_bias[depth_index][:, None, None, None], approximate=False).astype(jnp.bfloat16)
    final_bricks = global_bricks(grid, bricks_along_first, bricks_y, bricks_z)

    def decode_group(items):
        features, offsets, counts, local_part, global_part = items
        kernel_weight_value, unused_tiles = block_work(features, offsets, counts, local_part, bricks_y, bricks_z)
        return decode_points(jnp.take(final_bricks, global_part, axis=0), kernel_weight_value)

    decoded = lax.map(decode_group, stacked)
    return decoded.reshape((block_total,) + decoded.shape[2:])
```

```python
import functools
import math

import jax
import jax.numpy as jnp
from jax import lax
from jax.experimental import pallas as pl
from jax.experimental.pallas import tpu as pltpu
from jax.sharding import PartitionSpec as P

MODES = 32
NX = 128
NY = 128
NZ = 128
LAYERS = 2

AMPLITUDE = 0.25
SPREAD = 4.5
DECODE_SCALE = 0.1
VMEM_LIMIT = 60 * 1024 * 1024
F32 = jnp.float32
BF16 = jnp.bfloat16


def wave_numbers(kept_modes):
    position = jnp.arange(kept_modes, dtype=jnp.int32)
    return jnp.where(position < kept_modes // 2, position, position - kept_modes)


def forward_matrix(length, frequency):
    places = jnp.arange(length, dtype=jnp.int32)
    products = jnp.remainder(places[:, None] * frequency[None, :], length)
    angles = 2.0 * math.pi / length * products.astype(F32)
    cosine = jnp.cos(angles) / math.sqrt(length)
    sine_part = jnp.sin(angles) / math.sqrt(length)
    from_real = jnp.stack([cosine, -sine_part], axis=-1)
    from_imag = jnp.stack([sine_part, cosine], axis=-1)
    return jnp.stack([from_real, from_imag], axis=1)


def unit_angles(products, length):
    return 2.0 * math.pi / length * jnp.remainder(products, length).astype(F32)


def block_kernel(info_ref, slot, offsets, points):
    base = slot * 13
    count = info_ref[base + 12]
    lanes = lax.broadcasted_iota(jnp.int32, (1, points), 1)
    amplitude = jnp.where(lanes < count, AMPLITUDE, 0.0).astype(F32)

    def part(dim, brick, cells, scale):
        shift = ((info_ref[base + 3 * brick + dim] - info_ref[base + dim]) * scale).astype(F32)
        center = lax.broadcasted_iota(jnp.int32, (cells, points), 0).astype(F32) + 0.5
        apart = (offsets[dim : dim + 1, :] - shift) - center
        return jnp.exp(apart * apart * (-1.0 / SPREAD))

    rows = []
    for brick in range(4):
        along_x = part(0, brick, 2, 2) * amplitude
        along_y = part(1, brick, 4, 4)
        along_z = part(2, brick, 16, 16)
        for cy in range(4):
            plane = along_z * along_y[cy : cy + 1, :]
            rows.append(
                jnp.concatenate(
                    [plane * along_x[0:1, :], plane * along_x[1:2, :]], axis=1
                ).astype(BF16)
            )
    return jnp.concatenate(rows, axis=0)


def brick_place(info_ref, slot, brick, cy, depth):
    base = slot * 13 + 3 * brick
    row = (info_ref[base + 1] * 4 + cy) * depth + info_ref[base + 2] * 16
    return (
        pl.ds(pl.multiple_of(row, 16), 16),
        pl.ds(pl.multiple_of(info_ref[base] * 128, 128), 128),
    )


def encode_body(group, depth, steps, info_ref, feature_ref, offset_ref, out_ref, total_ref):
    step = pl.program_id(0)
    channels, points = feature_ref.shape[1:]

    @pl.when(step == 0)
    def _():
        total_ref[...] = jnp.zeros_like(total_ref)

    def one(member, carry):
        slot = step * group + member

        @pl.when(info_ref[slot * 13 + 12] > 0)
        def _():
            values = block_kernel(info_ref, slot, offset_ref[member].astype(F32), points)
            feature = feature_ref[member]
            empty = jnp.zeros_like(feature)
            pair = jnp.concatenate(
                [
                    jnp.concatenate([feature, empty], axis=1),
                    jnp.concatenate([empty, feature], axis=1),
                ],
                axis=0,
            )
            tiles = lax.dot_general(
                values, pair, (((1,), (1,)), ((), ())), preferred_element_type=F32
            )
            tiles = tiles.astype(BF16).astype(F32)
            for brick in range(4):
                for cy in range(4):
                    place = brick_place(info_ref, slot, brick, cy, depth)
                    start = brick * 64 + cy * 16
                    total_ref[place] = total_ref[place] + tiles[start : start + 16, :]

        return carry

    lax.fori_loop(0, group, one, 0)

    @pl.when(step == steps - 1)
    def _():
        out_ref[...] = total_ref[...].astype(BF16)


def encode(info, features, offsets, rows, depth, lanes):
    slots, channels, points = features.shape
    group = math.gcd(slots, 32)
    steps = slots // group
    return pl.pallas_call(
        functools.partial(encode_body, group, depth, steps),
        grid_spec=pltpu.PrefetchScalarGridSpec(
            num_scalar_prefetch=1,
            grid=(steps,),
            in_specs=[
                pl.BlockSpec((group, channels, points), lambda i, info: (i, 0, 0)),
                pl.BlockSpec((group, offsets.shape[1], points), lambda i, info: (i, 0, 0)),
            ],
            out_specs=pl.BlockSpec((rows, lanes), lambda i, info: (0, 0)),
            scratch_shapes=[pltpu.VMEM((rows, lanes), F32)],
        ),
        out_shape=jax.ShapeDtypeStruct((rows, lanes), BF16),
        compiler_params=pltpu.CompilerParams(vmem_limit_bytes=VMEM_LIMIT),
        name="encode",
    )(info, features, offsets)


def decode_body(group, depth, info_ref, grid_ref, offset_ref, out_ref):
    step = pl.program_id(0)
    channels, points = out_ref.shape[1:]

    def one(member, carry):
        slot = step * group + member

        @pl.when(info_ref[slot * 13 + 12] > 0)
        def _():
            values = block_kernel(info_ref, slot, offset_ref[member].astype(F32), points)
            cells = jnp.concatenate(
                [
                    grid_ref[brick_place(info_ref, slot, brick, cy, depth)]
                    for brick in range(4)
                    for cy in range(4)
                ],
                axis=0,
            )
            both = lax.dot_general(
                cells, values, (((0,), (0,)), ((), ())), preferred_element_type=F32
            )
            summed = both[:channels, :points] + both[channels:, points:]
            out_ref[member] = (DECODE_SCALE * summed).astype(BF16)

        @pl.when(info_ref[slot * 13 + 12] <= 0)
        def _():
            out_ref[member] = jnp.zeros((channels, points), BF16)

        return carry

    lax.fori_loop(0, group, one, 0)


def decode(info, grid, offsets, channels, depth):
    slots, rows3, points = offsets.shape
    group = math.gcd(slots, 32)
    return pl.pallas_call(
        functools.partial(decode_body, group, depth),
        grid_spec=pltpu.PrefetchScalarGridSpec(
            num_scalar_prefetch=1,
            grid=(slots // group,),
            in_specs=[
                pl.BlockSpec(grid.shape, lambda i, info: (0, 0)),
                pl.BlockSpec((group, rows3, points), lambda i, info: (i, 0, 0)),
            ],
            out_specs=pl.BlockSpec((group, channels, points), lambda i, info: (i, 0, 0)),
        ),
        out_shape=jax.ShapeDtypeStruct((slots, channels, points), BF16),
        compiler_params=pltpu.CompilerParams(vmem_limit_bytes=VMEM_LIMIT),
        name="decode",
    )(info, grid, offsets)


def forward_table_body(depth, u_ref, v_ref, cos_ref, sin_ref, out_ref):
    for place in range(out_ref.shape[1] // depth):
        out_ref[:, place * depth : (place + 1) * depth] = (
            u_ref[:, place : place + 1] * cos_ref[...] + v_ref[:, place : place + 1] * sin_ref[...]
        ).astype(BF16)


def forward_table(u, v, cosine, sine):
    modes, cells_y = u.shape
    depth = cosine.shape[1]
    block = math.gcd(modes, 256)
    narrow = pl.BlockSpec((block, cells_y), lambda i: (i, 0))
    wide = pl.BlockSpec((block, depth), lambda i: (i, 0))
    return pl.pallas_call(
        functools.partial(forward_table_body, depth),
        grid=(modes // block,),
        in_specs=[narrow, narrow, wide, wide],
        out_specs=pl.BlockSpec((block, cells_y * depth), lambda i: (i, 0)),
        out_shape=jax.ShapeDtypeStruct((modes, cells_y * depth), BF16),
        compiler_params=pltpu.CompilerParams(vmem_limit_bytes=VMEM_LIMIT),
        name="forward_table",
    )(u, v, cosine, sine)


def back_table_body(depth, u_ref, v_ref, cos_ref, sin_ref, out_ref):
    for place in range(u_ref.shape[0]):
        out_ref[place * depth : (place + 1) * depth, :] = (
            u_ref[place : place + 1, :] * cos_ref[...] + v_ref[place : place + 1, :] * sin_ref[...]
        ).astype(BF16)


def back_table(u, v, cosine, sine):
    cells_y, modes = u.shape
    depth = cosine.shape[0]
    group = math.gcd(cells_y, 8)
    narrow = pl.BlockSpec((group, modes), lambda i: (i, 0))
    wide = pl.BlockSpec((depth, modes), lambda i: (0, 0))
    return pl.pallas_call(
        functools.partial(back_table_body, depth),
        grid=(cells_y // group,),
        in_specs=[narrow, narrow, wide, wide],
        out_specs=pl.BlockSpec((group * depth, modes), lambda i: (i, 0)),
        out_shape=jax.ShapeDtypeStruct((cells_y * depth, modes), BF16),
        compiler_params=pltpu.CompilerParams(vmem_limit_bytes=VMEM_LIMIT),
        name="back_table",
    )(u, v, cosine, sine)


def layer_body(table_ref, modes_ref, grid_ref, skip_ref, bias_ref, out_ref):
    width = skip_ref.shape[0]
    for start in range(0, out_ref.shape[1], width):
        lanes = slice(start, start + width)
        spectral = jnp.dot(table_ref[...], modes_ref[:, lanes], preferred_element_type=F32)
        skipped = jnp.dot(grid_ref[:, lanes], skip_ref[...], preferred_element_type=F32)
        value = spectral + skipped + bias_ref[...]
        out_ref[:, lanes] = (
            0.5 * value * (1.0 + lax.erf(value * math.sqrt(0.5)))
        ).astype(BF16)


def layer_back(table, modes, grid, skip, bias):
    rows, lanes = grid.shape
    depth = modes.shape[0]
    block = math.gcd(rows, 256)
    channels = skip.shape[0]
    copies = math.gcd(lanes // channels, 4)
    width = copies * channels
    wide_skip = jnp.kron(jnp.eye(copies, dtype=BF16), skip)
    wide_bias = jnp.tile(bias, copies).reshape(1, width)
    return pl.pallas_call(
        layer_body,
        grid=(rows // block,),
        in_specs=[
            pl.BlockSpec((block, depth), lambda i: (i, 0)),
            pl.BlockSpec((depth, lanes), lambda i: (0, 0)),
            pl.BlockSpec((block, lanes), lambda i: (i, 0)),
            pl.BlockSpec((width, width), lambda i: (0, 0)),
            pl.BlockSpec((1, width), lambda i: (0, 0)),
        ],
        out_specs=pl.BlockSpec((block, lanes), lambda i: (i, 0)),
        out_shape=jax.ShapeDtypeStruct((rows, lanes), BF16),
        compiler_params=pltpu.CompilerParams(vmem_limit_bytes=VMEM_LIMIT),
        name="layer_back",
    )(table, modes, grid, wide_skip, wide_bias)


def swap(values, distance, size):
    return lax.ppermute(values, "py", [(i, i ^ distance) for i in range(size)])


def spectral_modes(grid, weights, forward, first_forward, first_back_table, size):
    rows_px = lax.axis_size("px")
    channels = weights.shape[3]
    ky_dev, kz_dev = weights.shape[1], weights.shape[2]
    lanes = grid.shape[1]
    x_dev = lanes // channels
    held = jnp.dot(forward, grid, preferred_element_type=F32).astype(BF16)
    held = held.reshape(size, -1, lanes)
    distance = 1
    while distance < size:
        halves = held.reshape(held.shape[0] // 2, 2, -1, lanes)
        came = swap(halves[:, 1], distance, size)
        held = (halves[:, 0].astype(F32) + came.astype(F32)).astype(BF16)
        distance *= 2
    own = held.reshape(rows_px, -1, lanes)
    lines = lax.all_to_all(own, "px", split_axis=0, concat_axis=0, tiled=True)
    lines = lines.reshape(rows_px, ky_dev, kz_dev, 2, x_dev, channels)
    first_modes = jnp.einsum(
        "skzpxc,sxpmq->mkzqc", lines, first_forward, preferred_element_type=F32
    ).astype(BF16)
    product = jnp.einsum(
        "mkzpc,mkzcr->mkzpr", first_modes, weights, preferred_element_type=F32
    )
    mixed = jnp.stack(
        [
            product[..., 0, :channels] - product[..., 1, channels:],
            product[..., 0, channels:] + product[..., 1, :channels],
        ],
        axis=3,
    ).astype(BF16)
    first_back = jnp.einsum(
        "mkzpc,mpsxq->skzqxc", mixed, first_back_table, preferred_element_type=F32
    ).astype(BF16)
    first_back = first_back.reshape(rows_px, -1, lanes)
    back = lax.all_to_all(first_back, "px", split_axis=0, concat_axis=0, tiled=True)
    held = back.reshape(1, -1, lanes)
    distance = size // 2
    while distance >= 1:
        came = swap(held, distance, size)
        held = jnp.stack([held, came], axis=1).reshape(-1, held.shape[1], lanes)
        distance //= 2
    return held.reshape(-1, lanes)


def slot_plan(block_bricks, bricks_device, slot_total, capacity):
    owners = block_bricks[:, 0] // bricks_device
    order_index = jnp.arange(owners.shape[0], dtype=jnp.int32)
    earlier = (owners[None, :] == owners[:, None]) & (order_index[None, :] < order_index[:, None])
    ranking = jnp.sum(earlier.astype(jnp.int32), axis=1)
    slot_index = owners * capacity + ranking
    matching = slot_index[None, :] == jnp.arange(slot_total, dtype=jnp.int32)[:, None]
    present = jnp.any(matching, axis=1)
    sources = jnp.sum(jnp.where(matching, order_index[None, :], 0), axis=1)
    return (slot_index, present, sources)


def pack_slots(values, present, sources, filler):
    picked = jnp.take(values, sources, axis=0)
    masking = present.reshape((-1,) + (1,) * (values.ndim - 1))
    return jnp.where(masking, picked, jnp.asarray(filler, values.dtype))


def route_back(values):
    return lax.all_to_all(values, ("px", "py"), split_axis=0, concat_axis=0, tiled=True)


def per_device(
    point_channel_values,
    point_offsets,
    point_counts,
    block_bricks,
    spectral_weights,
    skip_weights,
    skip_bias,
):
    mesh_rows = lax.axis_size("px")
    mesh_columns = lax.axis_size("py")
    device_total = mesh_rows * mesh_columns
    capacity = max(2, 2 * point_channel_values.shape[0] // device_total)
    channels, points = point_channel_values.shape[1:]
    x_dev, y_dev = NX // mesh_rows, NY // mesh_columns
    bricks_y = y_dev // 4
    bricks_z = NZ // 16
    bricks_device = x_dev // 2 * bricks_y * bricks_z
    slot_total = device_total * capacity
    local_ids = block_bricks % bricks_device
    slot_index, present, sources = slot_plan(block_bricks, bricks_device, slot_total, capacity)
    coordinates = jnp.stack(
        [local_ids // (bricks_y * bricks_z), local_ids // bricks_z % bricks_y, local_ids % bricks_z],
        axis=-1,
    ).reshape(local_ids.shape[0], -1)
    facts = jnp.concatenate([coordinates, point_counts[:, None]], axis=1).astype(BF16)
    facts = jnp.pad(facts, ((0, 0), (0, points - facts.shape[1])))
    notes = jnp.concatenate([point_offsets, facts[:, None, :]], axis=1)
    packed_notes = pack_slots(notes, present, sources, 0)
    packed_features = pack_slots(point_channel_values, present, sources, 0)
    got_notes = route_back(packed_notes)
    got_features = route_back(packed_features)
    info = got_notes[:, 3, :13].astype(jnp.int32).reshape(-1)

    kz_dev = MODES // mesh_columns
    me_x, me_y = lax.axis_index("px"), lax.axis_index("py")
    index = jnp.arange(2 * MODES * MODES, dtype=jnp.int32)
    part = index % 2
    kz = index // 2 % kz_dev + kz_dev * jnp.bitwise_xor(index // (2 * kz_dev * MODES), me_y)
    ky_at = index // (2 * kz_dev) % MODES
    ky = jnp.where(ky_at < MODES // 2, ky_at, ky_at - MODES)
    angle_y = unit_angles(
        ky[:, None] * (me_y * y_dev + jnp.arange(y_dev, dtype=jnp.int32))[None, :], NY
    )
    angle_z = unit_angles(kz[:, None] * jnp.arange(NZ, dtype=jnp.int32)[None, :], NZ)
    real_row = (part == 0)[:, None]
    norm = 1.0 / math.sqrt(NY * NZ)
    cos_y, sin_y = jnp.cos(angle_y) * norm, jnp.sin(angle_y) * norm
    table_u = jnp.where(real_row, cos_y, -sin_y)
    table_v = jnp.where(real_row, -sin_y, -cos_y)
    cos_z, sin_z = jnp.cos(angle_z), jnp.sin(angle_z)
    forward = forward_table(table_u, table_v, cos_z, sin_z)
    fold = jnp.where(kz == 0, 1.0, 2.0).astype(F32)[:, None]
    back = back_table(table_u.T, table_v.T, (cos_z * fold).T, (sin_z * fold).T)
    first_matrix = forward_matrix(NX, wave_numbers(MODES))
    first_forward = first_matrix.reshape(mesh_rows, x_dev, 2, MODES, 2).astype(BF16)
    first_back = (
        first_matrix.transpose(2, 3, 0, 1).reshape(MODES, 2, mesh_rows, x_dev, 2).astype(BF16)
    )
    grid = encode(info, got_features, got_notes, y_dev * NZ, NZ, x_dev * channels)
    for depth_index in range(LAYERS):
        modes = spectral_modes(
            grid, spectral_weights[depth_index], forward, first_forward, first_back, mesh_columns
        )
        grid = layer_back(
            back, modes, grid, skip_weights[depth_index], skip_bias[depth_index]
        )
    reply = decode(info, grid, got_notes, channels, NZ)
    returned = route_back(reply)
    return jnp.take(returned, slot_index, axis=0)


def solution(mesh):
    return jax.shard_map(
        per_device,
        mesh=mesh,
        in_specs=(
            P(("px", "py"), None, None),
            P(("px", "py"), None, None),
            P(("px", "py")),
            P(("px", "py"), None),
            P(None, None, "px", "py", None, None),
            P(),
            P(),
        ),
        out_specs=P(("px", "py"), None, None),
        check_vma=False,
    )
```

```python
import functools
import math

import jax
import jax.numpy as jnp
from jax import lax
from jax.experimental import pallas as pl
from jax.experimental.pallas import tpu as pltpu
from jax.sharding import PartitionSpec as P

MODES = 32
NX = 128
NY = 128
NZ = 128
LAYERS = 2

AMPLITUDE = 0.25
SPREAD = 4.5
DECODE_SCALE = 0.1
CHUNKS = 2
WAYS = 4
VMEM_LIMIT = 60 * 1024 * 1024
F32 = jnp.float32
BF16 = jnp.bfloat16


def wave_numbers(kept_modes):
    position = jnp.arange(kept_modes, dtype=jnp.int32)
    return jnp.where(position < kept_modes // 2, position, position - kept_modes)


def forward_matrix(length, frequency):
    places = jnp.arange(length, dtype=jnp.int32)
    products = jnp.remainder(places[:, None] * frequency[None, :], length)
    angles = 2.0 * math.pi / length * products.astype(F32)
    cosine = jnp.cos(angles) / math.sqrt(length)
    sine_part = jnp.sin(angles) / math.sqrt(length)
    from_real = jnp.stack([cosine, -sine_part], axis=-1)
    from_imag = jnp.stack([sine_part, cosine], axis=-1)
    return jnp.stack([from_real, from_imag], axis=1)


def unit_angles(products, length):
    return 2.0 * math.pi / length * jnp.remainder(products, length).astype(F32)


def block_kernel(info_ref, slot, offsets, points):
    base = slot * 13
    count = info_ref[base + 12]
    lanes = lax.broadcasted_iota(jnp.int32, (1, points), 1)
    amplitude = jnp.where(lanes < count, AMPLITUDE, 0.0).astype(F32)

    def part(dim, brick, cells, scale):
        shift = ((info_ref[base + 3 * brick + dim] - info_ref[base + dim]) * scale).astype(F32)
        center = lax.broadcasted_iota(jnp.int32, (cells, points), 0).astype(F32) + 0.5
        apart = (offsets[dim : dim + 1, :] - shift) - center
        return jnp.exp(apart * apart * (-1.0 / SPREAD))

    rows = []
    for brick in range(4):
        along_x = part(0, brick, 2, 2) * amplitude
        along_y = part(1, brick, 4, 4)
        along_z = part(2, brick, 16, 16)
        for cy in range(4):
            plane = along_z * along_y[cy : cy + 1, :]
            rows.append(
                jnp.concatenate(
                    [plane * along_x[0:1, :], plane * along_x[1:2, :]], axis=1
                ).astype(BF16)
            )
    return jnp.concatenate(rows, axis=0)


def brick_place(info_ref, slot, brick, cy, depth):
    base = slot * 13 + 3 * brick
    row = (info_ref[base + 1] * 4 + cy) * depth + info_ref[base + 2] * 16
    return (
        pl.ds(pl.multiple_of(row, 16), 16),
        pl.ds(pl.multiple_of(info_ref[base] * 128, 128), 128),
    )


def encode_body(group, depth, steps, info_ref, feature_ref, offset_ref, *refs):
    out_refs, total_ref = refs[:-1], refs[-1]
    step = pl.program_id(0)

    @pl.when(step == 0)
    def _():
        total_ref[...] = jnp.zeros_like(total_ref)

    def some(turn, carry):
        tiles = []
        for way in range(WAYS):
            member = turn * WAYS + way
            values = block_kernel(
                info_ref, step * group + member, offset_ref[member].astype(F32), offset_ref.shape[2]
            )
            feature = feature_ref[member]
            empty = jnp.zeros_like(feature)
            pair = jnp.concatenate(
                [
                    jnp.concatenate([feature, empty], axis=1),
                    jnp.concatenate([empty, feature], axis=1),
                ],
                axis=0,
            )
            tiles.append(
                lax.dot_general(values, pair, (((1,), (1,)), ((), ())), preferred_element_type=F32)
            )
        for way in range(WAYS):
            slot = step * group + turn * WAYS + way
            rounded = tiles[way].astype(BF16).astype(F32)
            places = [
                brick_place(info_ref, slot, brick, cy, depth)
                for brick in range(4)
                for cy in range(4)
            ]
            sums = [
                total_ref[place] + rounded[16 * at : 16 * at + 16, :]
                for at, place in enumerate(places)
            ]
            used = info_ref[slot * 13 + 12] > 0

            @pl.when(used)
            def _():
                for place, value in zip(places, sums):
                    total_ref[place] = value

        return carry

    lax.fori_loop(0, group // WAYS, some, 0)

    @pl.when(step == steps - 1)
    def _():
        for at, out_ref in enumerate(out_refs):
            width = out_ref.shape[1]
            out_ref[...] = total_ref[:, at * width : (at + 1) * width].astype(BF16)


def encode(info, features, offsets, rows, depth, lanes):
    slots, channels, points = features.shape
    group = math.gcd(slots, 32)
    steps = slots // group
    width = lanes // CHUNKS
    return pl.pallas_call(
        functools.partial(encode_body, group, depth, steps),
        grid_spec=pltpu.PrefetchScalarGridSpec(
            num_scalar_prefetch=1,
            grid=(steps,),
            in_specs=[
                pl.BlockSpec((group, channels, points), lambda i, info: (i, 0, 0)),
                pl.BlockSpec((group, offsets.shape[1], points), lambda i, info: (i, 0, 0)),
            ],
            out_specs=[pl.BlockSpec((rows, width), lambda i, info: (0, 0))] * CHUNKS,
            scratch_shapes=[pltpu.VMEM((rows, lanes), F32)],
        ),
        out_shape=[jax.ShapeDtypeStruct((rows, width), BF16)] * CHUNKS,
        compiler_params=pltpu.CompilerParams(vmem_limit_bytes=VMEM_LIMIT),
        name="encode",
    )(info, features, offsets)


def decode_body(group, depth, info_ref, *refs):
    grid_refs, offset_ref, out_ref, held_ref = refs[:CHUNKS], refs[-3], refs[-2], refs[-1]
    step = pl.program_id(0)
    channels, points = out_ref.shape[1:]

    @pl.when(step == 0)
    def _():
        for at, grid_ref in enumerate(grid_refs):
            width = grid_ref.shape[1]
            held_ref[:, at * width : (at + 1) * width] = grid_ref[...]

    def some(turn, carry):
        results = []
        for way in range(WAYS):
            member = turn * WAYS + way
            slot = step * group + member
            values = block_kernel(info_ref, slot, offset_ref[member].astype(F32), points)
            cells = jnp.concatenate(
                [
                    held_ref[brick_place(info_ref, slot, brick, cy, depth)]
                    for brick in range(4)
                    for cy in range(4)
                ],
                axis=0,
            )
            both = lax.dot_general(
                cells, values, (((0,), (0,)), ((), ())), preferred_element_type=F32
            )
            summed = both[:channels, :points] + both[channels:, points:]
            results.append((DECODE_SCALE * summed).astype(BF16))
        for way in range(WAYS):
            out_ref[turn * WAYS + way] = results[way]
        return carry

    lax.fori_loop(0, group // WAYS, some, 0)


def decode(info, grids, offsets, channels, depth):
    slots, rows3, points = offsets.shape
    group = math.gcd(slots, 32)
    rows, width = grids[0].shape
    return pl.pallas_call(
        functools.partial(decode_body, group, depth),
        grid_spec=pltpu.PrefetchScalarGridSpec(
            num_scalar_prefetch=1,
            grid=(slots // group,),
            in_specs=[pl.BlockSpec((rows, width), lambda i, info: (0, 0))] * CHUNKS
            + [pl.BlockSpec((group, rows3, points), lambda i, info: (i, 0, 0))],
            out_specs=pl.BlockSpec((group, channels, points), lambda i, info: (i, 0, 0)),
            scratch_shapes=[pltpu.VMEM((rows, width * CHUNKS), BF16)],
        ),
        out_shape=jax.ShapeDtypeStruct((slots, channels, points), BF16),
        compiler_params=pltpu.CompilerParams(vmem_limit_bytes=VMEM_LIMIT),
        name="decode",
    )(info, *grids, offsets)


def forward_table_body(depth, u_ref, v_ref, cos_ref, sin_ref, out_ref):
    for place in range(out_ref.shape[1] // depth):
        out_ref[:, place * depth : (place + 1) * depth] = (
            u_ref[:, place : place + 1] * cos_ref[...] + v_ref[:, place : place + 1] * sin_ref[...]
        ).astype(BF16)


def forward_table(u, v, cosine, sine):
    modes, cells_y = u.shape
    depth = cosine.shape[1]
    block = math.gcd(modes, 256)
    narrow = pl.BlockSpec((block, cells_y), lambda i: (i, 0))
    wide = pl.BlockSpec((block, depth), lambda i: (i, 0))
    return pl.pallas_call(
        functools.partial(forward_table_body, depth),
        grid=(modes // block,),
        in_specs=[narrow, narrow, wide, wide],
        out_specs=pl.BlockSpec((block, cells_y * depth), lambda i: (i, 0)),
        out_shape=jax.ShapeDtypeStruct((modes, cells_y * depth), BF16),
        compiler_params=pltpu.CompilerParams(vmem_limit_bytes=VMEM_LIMIT),
        name="forward_table",
    )(u, v, cosine, sine)


def back_table_body(depth, u_ref, v_ref, cos_ref, sin_ref, out_ref):
    for place in range(u_ref.shape[0]):
        out_ref[place * depth : (place + 1) * depth, :] = (
            u_ref[place : place + 1, :] * cos_ref[...] + v_ref[place : place + 1, :] * sin_ref[...]
        ).astype(BF16)


def back_table(u, v, cosine, sine):
    cells_y, modes = u.shape
    depth = cosine.shape[0]
    group = math.gcd(cells_y, 8)
    narrow = pl.BlockSpec((group, modes), lambda i: (i, 0))
    wide = pl.BlockSpec((depth, modes), lambda i: (0, 0))
    return pl.pallas_call(
        functools.partial(back_table_body, depth),
        grid=(cells_y // group,),
        in_specs=[narrow, narrow, wide, wide],
        out_specs=pl.BlockSpec((group * depth, modes), lambda i: (i, 0)),
        out_shape=jax.ShapeDtypeStruct((cells_y * depth, modes), BF16),
        compiler_params=pltpu.CompilerParams(vmem_limit_bytes=VMEM_LIMIT),
        name="back_table",
    )(u, v, cosine, sine)


def layer_body(table_ref, modes_ref, grid_ref, skip_ref, bias_ref, out_ref):
    width = skip_ref.shape[0]
    for start in range(0, out_ref.shape[1], width):
        lanes = slice(start, start + width)
        spectral = jnp.dot(table_ref[...], modes_ref[:, lanes], preferred_element_type=F32)
        skipped = jnp.dot(grid_ref[:, lanes], skip_ref[...], preferred_element_type=F32)
        value = spectral + skipped + bias_ref[...]
        out_ref[:, lanes] = (
            0.5 * value * (1.0 + lax.erf(value * math.sqrt(0.5)))
        ).astype(BF16)


def skip_tables(skip, bias, width):
    copies = width // skip.shape[0]
    same = jnp.eye(copies, dtype=bool)[:, None, :, None]
    wide = jnp.where(same, skip[None, :, None, :], jnp.zeros((), skip.dtype))
    return wide.reshape(width, width), jnp.tile(bias, copies).reshape(1, width)


def layer_back(table, modes, grid, wide_skip, wide_bias):
    rows, lanes = grid.shape
    depth = modes.shape[0]
    block = math.gcd(rows, 512)
    width = wide_skip.shape[0]
    return pl.pallas_call(
        layer_body,
        grid=(rows // block,),
        in_specs=[
            pl.BlockSpec((block, depth), lambda i: (i, 0)),
            pl.BlockSpec((depth, lanes), lambda i: (0, 0)),
            pl.BlockSpec((block, lanes), lambda i: (i, 0)),
            pl.BlockSpec((width, width), lambda i: (0, 0)),
            pl.BlockSpec((1, width), lambda i: (0, 0)),
        ],
        out_specs=pl.BlockSpec((block, lanes), lambda i: (i, 0)),
        out_shape=jax.ShapeDtypeStruct((rows, lanes), BF16),
        compiler_params=pltpu.CompilerParams(vmem_limit_bytes=40 * 1024 * 1024),
        cost_estimate=pl.CostEstimate(
            flops=2 * rows * lanes * (depth + width),
            bytes_accessed=2 * rows * (depth + 2 * lanes),
            transcendentals=rows * lanes,
        ),
        name="layer_back",
    )(table, modes, grid, wide_skip, wide_bias)


def swap(values, distance, size):
    return lax.ppermute(values, "py", [(i, i ^ distance) for i in range(size)])


def reduced_modes(grid, forward, size):
    lanes = grid.shape[1]
    held = jnp.dot(forward, grid, preferred_element_type=F32).astype(BF16)
    held = held.reshape(size, -1, lanes)
    distance = 1
    while distance < size:
        halves = held.reshape(held.shape[0] // 2, 2, -1, lanes)
        came = swap(halves[:, 1], distance, size)
        held = (halves[:, 0].astype(F32) + came.astype(F32)).astype(BF16)
        distance *= 2
    return held


def gathered_modes(held, size):
    distance = size // 2
    while distance >= 1:
        came = swap(held, distance, size)
        held = jnp.stack([held, came], axis=1).reshape(-1, held.shape[1], held.shape[2])
        distance //= 2
    return held.reshape(-1, held.shape[2])


def exchange_x(values):
    return lax.all_to_all(values, "px", split_axis=0, concat_axis=0, tiled=True)


def spectral_modes(grids, weights, forward, first_forward, first_back_table, size):
    rows_px = lax.axis_size("px")
    channels = weights.shape[3]
    ky_dev, kz_dev = weights.shape[1], weights.shape[2]
    lanes = grids[0].shape[1]
    x_chunk = lanes // channels
    first_modes = 0.0
    for at, grid in enumerate(grids):
        own = reduced_modes(grid, forward, size).reshape(rows_px, -1, lanes)
        lines = exchange_x(own).reshape(rows_px, ky_dev, kz_dev, 2, x_chunk, channels)
        first_modes += jnp.einsum(
            "skzpxc,sxpmq->mkzqc",
            lines,
            first_forward[:, at * x_chunk : (at + 1) * x_chunk],
            preferred_element_type=F32,
        )
    product = jnp.einsum(
        "mkzpc,mkzcr->mkzpr", first_modes.astype(BF16), weights, preferred_element_type=F32
    )
    mixed = jnp.stack(
        [
            product[..., 0, :channels] - product[..., 1, channels:],
            product[..., 0, channels:] + product[..., 1, :channels],
        ],
        axis=3,
    ).astype(BF16)
    modes = []
    for at in range(len(grids)):
        first_back = jnp.einsum(
            "mkzpc,mpsxq->skzqxc",
            mixed,
            first_back_table[:, :, :, at * x_chunk : (at + 1) * x_chunk],
            preferred_element_type=F32,
        ).astype(BF16)
        back = exchange_x(first_back.reshape(rows_px, -1, lanes))
        modes.append(gathered_modes(back.reshape(1, -1, lanes), size))
    return modes


def slot_plan(block_bricks, bricks_device, slot_total, capacity):
    owners = block_bricks[:, 0] // bricks_device
    order_index = jnp.arange(owners.shape[0], dtype=jnp.int32)
    earlier = (owners[None, :] == owners[:, None]) & (order_index[None, :] < order_index[:, None])
    ranking = jnp.sum(earlier.astype(jnp.int32), axis=1)
    slot_index = owners * capacity + ranking
    matching = slot_index[None, :] == jnp.arange(slot_total, dtype=jnp.int32)[:, None]
    present = jnp.any(matching, axis=1)
    sources = jnp.sum(jnp.where(matching, order_index[None, :], 0), axis=1)
    return (slot_index, present, sources)


def pack_slots(values, present, sources, filler):
    picked = jnp.take(values, sources, axis=0)
    masking = present.reshape((-1,) + (1,) * (values.ndim - 1))
    return jnp.where(masking, picked, jnp.asarray(filler, values.dtype))


def route_back(values):
    return lax.all_to_all(values, ("px", "py"), split_axis=0, concat_axis=0, tiled=True)


def per_device(
    point_channel_values,
    point_offsets,
    point_counts,
    block_bricks,
    spectral_weights,
    skip_weights,
    skip_bias,
):
    mesh_rows = lax.axis_size("px")
    mesh_columns = lax.axis_size("py")
    device_total = mesh_rows * mesh_columns
    capacity = max(2, 2 * point_channel_values.shape[0] // device_total)
    channels, points = point_channel_values.shape[1:]
    x_dev, y_dev = NX // mesh_rows, NY // mesh_columns
    bricks_y = y_dev // 4
    bricks_z = NZ // 16
    bricks_device = x_dev // 2 * bricks_y * bricks_z
    slot_total = device_total * capacity
    local_ids = block_bricks % bricks_device
    slot_index, present, sources = slot_plan(block_bricks, bricks_device, slot_total, capacity)
    coordinates = jnp.stack(
        [local_ids // (bricks_y * bricks_z), local_ids // bricks_z % bricks_y, local_ids % bricks_z],
        axis=-1,
    ).reshape(local_ids.shape[0], -1)
    facts = jnp.concatenate([coordinates, point_counts[:, None]], axis=1).astype(BF16)
    facts = jnp.pad(facts, ((0, 0), (0, points - facts.shape[1])))
    notes = jnp.concatenate([point_offsets, facts[:, None, :]], axis=1)
    packed_notes = pack_slots(notes, present, sources, 0)
    packed_features = pack_slots(point_channel_values, present, sources, 0)
    got_notes = route_back(packed_notes)
    got_features = route_back(packed_features)
    info = got_notes[:, 3, :13].astype(jnp.int32).reshape(-1)

    kz_dev = MODES // mesh_columns
    me_x, me_y = lax.axis_index("px"), lax.axis_index("py")
    index = jnp.arange(2 * MODES * MODES, dtype=jnp.int32)
    part = index % 2
    kz = index // 2 % kz_dev + kz_dev * jnp.bitwise_xor(index // (2 * kz_dev * MODES), me_y)
    ky_at = index // (2 * kz_dev) % MODES
    ky = jnp.where(ky_at < MODES // 2, ky_at, ky_at - MODES)
    angle_y = unit_angles(
        ky[:, None] * (me_y * y_dev + jnp.arange(y_dev, dtype=jnp.int32))[None, :], NY
    )
    angle_z = unit_angles(kz[:, None] * jnp.arange(NZ, dtype=jnp.int32)[None, :], NZ)
    real_row = (part == 0)[:, None]
    norm = 1.0 / math.sqrt(NY * NZ)
    cos_y, sin_y = jnp.cos(angle_y) * norm, jnp.sin(angle_y) * norm
    table_u = jnp.where(real_row, cos_y, -sin_y)
    table_v = jnp.where(real_row, -sin_y, -cos_y)
    cos_z, sin_z = jnp.cos(angle_z), jnp.sin(angle_z)
    forward = forward_table(table_u, table_v, cos_z, sin_z)
    fold = jnp.where(kz == 0, 1.0, 2.0).astype(F32)[:, None]
    back = back_table(table_u.T, table_v.T, (cos_z * fold).T, (sin_z * fold).T)
    first_matrix = forward_matrix(NX, wave_numbers(MODES))
    first_forward = first_matrix.reshape(mesh_rows, x_dev, 2, MODES, 2).astype(BF16)
    first_back = (
        first_matrix.transpose(2, 3, 0, 1).reshape(MODES, 2, mesh_rows, x_dev, 2).astype(BF16)
    )
    lanes = x_dev * channels
    width = math.gcd(lanes // CHUNKS, 4 * channels)
    skips = [skip_tables(skip_weights[at], skip_bias[at], width) for at in range(LAYERS)]
    got_features, forward, back, first_forward, first_back, skips = lax.optimization_barrier(
        (got_features, forward, back, first_forward, first_back, skips)
    )
    grids = encode(info, got_features, got_notes, y_dev * NZ, NZ, lanes)
    for depth_index in range(LAYERS):
        modes = spectral_modes(
            grids, spectral_weights[depth_index], forward, first_forward, first_back, mesh_columns
        )
        grids = [
            layer_back(back, mode, grid, *skips[depth_index]) for mode, grid in zip(modes, grids)
        ]
    reply = decode(info, grids, got_notes, channels, NZ)
    returned = route_back(reply)
    return jnp.take(returned, slot_index, axis=0)


def solution(mesh):
    return jax.shard_map(
        per_device,
        mesh=mesh,
        in_specs=(
            P(("px", "py"), None, None),
            P(("px", "py"), None, None),
            P(("px", "py")),
            P(("px", "py"), None),
            P(None, None, "px", "py", None, None),
            P(),
            P(),
        ),
        out_specs=P(("px", "py"), None, None),
        check_vma=False,
    )
```

```python
import functools
import math

import jax
import jax.numpy as jnp
from jax import lax
from jax.experimental import pallas as pl
from jax.experimental.pallas import tpu as pltpu
from jax.sharding import PartitionSpec as P

MODES = 32
NX = 128
NY = 128
NZ = 128
LAYERS = 2

AMPLITUDE = 0.25
SPREAD = 4.5
DECODE_SCALE = 0.1
CHUNKS = 2
WAYS = 4
VMEM_LIMIT = 60 * 1024 * 1024
F32 = jnp.float32
BF16 = jnp.bfloat16


def wave_numbers(kept_modes):
    position = jnp.arange(kept_modes, dtype=jnp.int32)
    return jnp.where(position < kept_modes // 2, position, position - kept_modes)


def forward_matrix(length, frequency):
    places = jnp.arange(length, dtype=jnp.int32)
    products = jnp.remainder(places[:, None] * frequency[None, :], length)
    angles = 2.0 * math.pi / length * products.astype(F32)
    cosine = jnp.cos(angles) / math.sqrt(length)
    sine_part = jnp.sin(angles) / math.sqrt(length)
    from_real = jnp.stack([cosine, -sine_part], axis=-1)
    from_imag = jnp.stack([sine_part, cosine], axis=-1)
    return jnp.stack([from_real, from_imag], axis=1)


def unit_angles(products, length):
    return 2.0 * math.pi / length * jnp.remainder(products, length).astype(F32)


def block_kernel(info_ref, slot, offsets, points):
    base = slot * 13
    count = info_ref[base + 12]
    lanes = lax.broadcasted_iota(jnp.int32, (1, points), 1)
    amplitude = jnp.where(lanes < count, AMPLITUDE, 0.0).astype(F32)

    def part(dim, brick, cells, scale):
        shift = ((info_ref[base + 3 * brick + dim] - info_ref[base + dim]) * scale).astype(F32)
        center = lax.broadcasted_iota(jnp.int32, (cells, points), 0).astype(F32) + 0.5
        apart = (offsets[dim : dim + 1, :] - shift) - center
        return jnp.exp(apart * apart * (-1.0 / SPREAD))

    rows = []
    for brick in range(4):
        along_x = part(0, brick, 2, 2) * amplitude
        along_y = part(1, brick, 4, 4)
        along_z = part(2, brick, 16, 16)
        for cy in range(4):
            plane = along_z * along_y[cy : cy + 1, :]
            rows.append(
                jnp.concatenate(
                    [plane * along_x[0:1, :], plane * along_x[1:2, :]], axis=1
                ).astype(BF16)
            )
    return jnp.concatenate(rows, axis=0)


def brick_place(info_ref, slot, brick, cy, depth):
    base = slot * 13 + 3 * brick
    row = (info_ref[base + 1] * 4 + cy) * depth + info_ref[base + 2] * 16
    return (
        pl.ds(pl.multiple_of(row, 16), 16),
        pl.ds(pl.multiple_of(info_ref[base] * 128, 128), 128),
    )


def encode_body(group, depth, steps, info_ref, feature_ref, offset_ref, *refs):
    out_refs, total_ref = refs[:-1], refs[-1]
    step = pl.program_id(0)

    @pl.when(step == 0)
    def _():
        total_ref[...] = jnp.zeros_like(total_ref)

    def some(turn, carry):
        tiles = []
        for way in range(WAYS):
            member = turn * WAYS + way
            values = block_kernel(
                info_ref, step * group + member, offset_ref[member].astype(F32), offset_ref.shape[2]
            )
            feature = feature_ref[member]
            empty = jnp.zeros_like(feature)
            pair = jnp.concatenate(
                [
                    jnp.concatenate([feature, empty], axis=1),
                    jnp.concatenate([empty, feature], axis=1),
                ],
                axis=0,
            )
            tiles.append(
                lax.dot_general(values, pair, (((1,), (1,)), ((), ())), preferred_element_type=F32)
            )
        for way in range(WAYS):
            slot = step * group + turn * WAYS + way
            rounded = tiles[way].astype(BF16).astype(F32)
            places = [
                brick_place(info_ref, slot, brick, cy, depth)
                for brick in range(4)
                for cy in range(4)
            ]
            sums = [
                total_ref[place] + rounded[16 * at : 16 * at + 16, :]
                for at, place in enumerate(places)
            ]
            for place, value in zip(places, sums):
                total_ref[place] = value

        return carry

    lax.fori_loop(0, group // WAYS, some, 0)

    @pl.when(step == steps - 1)
    def _():
        for at, out_ref in enumerate(out_refs):
            width = out_ref.shape[1]
            out_ref[...] = total_ref[:, at * width : (at + 1) * width].astype(BF16)


def encode(info, features, offsets, rows, depth, lanes):
    slots, channels, points = features.shape
    group = math.gcd(slots, 32)
    steps = slots // group
    width = lanes // CHUNKS
    return pl.pallas_call(
        functools.partial(encode_body, group, depth, steps),
        grid_spec=pltpu.PrefetchScalarGridSpec(
            num_scalar_prefetch=1,
            grid=(steps,),
            in_specs=[
                pl.BlockSpec((group, channels, points), lambda i, info: (i, 0, 0)),
                pl.BlockSpec((group, offsets.shape[1], points), lambda i, info: (i, 0, 0)),
            ],
            out_specs=[pl.BlockSpec((rows, width), lambda i, info: (0, 0))] * CHUNKS,
            scratch_shapes=[pltpu.VMEM((rows, lanes), F32)],
        ),
        out_shape=[jax.ShapeDtypeStruct((rows, width), BF16)] * CHUNKS,
        compiler_params=pltpu.CompilerParams(vmem_limit_bytes=VMEM_LIMIT),
        name="encode",
    )(info, features, offsets)


def decode_body(group, depth, info_ref, *refs):
    grid_refs, offset_ref, out_ref, held_ref = refs[:CHUNKS], refs[-3], refs[-2], refs[-1]
    step = pl.program_id(0)
    channels, points = out_ref.shape[1:]

    @pl.when(step == 0)
    def _():
        for at, grid_ref in enumerate(grid_refs):
            width = grid_ref.shape[1]
            held_ref[:, at * width : (at + 1) * width] = grid_ref[...]

    def some(turn, carry):
        results = []
        for way in range(WAYS):
            member = turn * WAYS + way
            slot = step * group + member
            values = block_kernel(info_ref, slot, offset_ref[member].astype(F32), points)
            cells = jnp.concatenate(
                [
                    held_ref[brick_place(info_ref, slot, brick, cy, depth)]
                    for brick in range(4)
                    for cy in range(4)
                ],
                axis=0,
            )
            both = lax.dot_general(
                cells, values, (((0,), (0,)), ((), ())), preferred_element_type=F32
            )
            summed = both[:channels, :points] + both[channels:, points:]
            results.append((DECODE_SCALE * summed).astype(BF16))
        for way in range(WAYS):
            out_ref[turn * WAYS + way] = results[way]
        return carry

    lax.fori_loop(0, group // WAYS, some, 0)


def decode(info, grids, offsets, channels, depth):
    slots, rows3, points = offsets.shape
    group = math.gcd(slots, 32)
    rows, width = grids[0].shape
    return pl.pallas_call(
        functools.partial(decode_body, group, depth),
        grid_spec=pltpu.PrefetchScalarGridSpec(
            num_scalar_prefetch=1,
            grid=(slots // group,),
            in_specs=[pl.BlockSpec((rows, width), lambda i, info: (0, 0))] * CHUNKS
            + [pl.BlockSpec((group, rows3, points), lambda i, info: (i, 0, 0))],
            out_specs=pl.BlockSpec((group, channels, points), lambda i, info: (i, 0, 0)),
            scratch_shapes=[pltpu.VMEM((rows, width * CHUNKS), BF16)],
        ),
        out_shape=jax.ShapeDtypeStruct((slots, channels, points), BF16),
        compiler_params=pltpu.CompilerParams(vmem_limit_bytes=VMEM_LIMIT),
        name="decode",
    )(info, *grids, offsets)


def forward_body(groups, third_ref, second_ref, grid_ref, out_ref, held_ref):
    depth = third_ref.shape[1]
    span = third_ref.shape[0] // groups
    cells_y = grid_ref.shape[0] // depth
    count_in, count_out = second_ref.shape[1], second_ref.shape[0]

    def some(turn, carry):
        for way in range(WAYS):
            y = turn * WAYS + way
            line = grid_ref[pl.ds(pl.multiple_of(y * depth, depth), depth), :]
            modes = jnp.dot(third_ref[...], line, preferred_element_type=F32)
            for at in range(groups):
                row = pl.multiple_of(at * count_in + y * span, span)
                held_ref[pl.ds(row, span), :] = modes[at * span : (at + 1) * span, :]
        return carry

    lax.fori_loop(0, cells_y // WAYS, some, 0)
    for at in range(groups):
        third = held_ref[at * count_in : (at + 1) * count_in, :].astype(BF16)
        out_ref[at * count_out : (at + 1) * count_out, :] = jnp.dot(
            second_ref[...], third, preferred_element_type=F32
        ).astype(BF16)


def forward_modes(third, second, grid, groups):
    rows, lanes = grid.shape
    count_out, count_in = second.shape
    width = math.gcd(lanes, 256)
    return pl.pallas_call(
        functools.partial(forward_body, groups),
        grid=(lanes // width,),
        in_specs=[
            pl.BlockSpec(third.shape, lambda i: (0, 0)),
            pl.BlockSpec(second.shape, lambda i: (0, 0)),
            pl.BlockSpec((rows, width), lambda i: (0, i)),
        ],
        out_specs=pl.BlockSpec((groups * count_out, width), lambda i: (0, i)),
        out_shape=jax.ShapeDtypeStruct((groups * count_out, lanes), BF16),
        scratch_shapes=[pltpu.VMEM((groups * count_in, width), F32)],
        compiler_params=pltpu.CompilerParams(vmem_limit_bytes=40 * 1024 * 1024),
        cost_estimate=pl.CostEstimate(
            flops=8 * groups * lanes * count_out * count_in,
            bytes_accessed=2 * lanes * (rows + groups * count_out),
            transcendentals=0,
        ),
        name="forward_modes",
    )(third, second, grid)


def layer_body(groups, second_ref, third_ref, modes_ref, grid_ref, skip_ref, bias_ref, out_ref, held_ref):
    depth = third_ref.shape[0]
    span = third_ref.shape[1] // groups
    cells_y = grid_ref.shape[0] // depth
    count_out, count_in = second_ref.shape
    for at in range(groups):
        held_ref[at * count_out : (at + 1) * count_out, :] = jnp.dot(
            second_ref[...],
            modes_ref[at * count_in : (at + 1) * count_in, :],
            preferred_element_type=F32,
        )

    def some(turn, carry):
        for way in range(2):
            y = turn * 2 + way
            pieces = []
            for at in range(groups):
                row = pl.multiple_of(at * count_out + y * span, span)
                pieces.append(held_ref[pl.ds(row, span), :])
            line = jnp.concatenate(pieces, axis=0).astype(BF16)
            place = pl.ds(pl.multiple_of(y * depth, depth), depth)
            spectral = jnp.dot(third_ref[...], line, preferred_element_type=F32)
            skipped = jnp.dot(grid_ref[place, :], skip_ref[...], preferred_element_type=F32)
            value = spectral + skipped + bias_ref[...]
            out_ref[place, :] = (0.5 * value * (1.0 + lax.erf(value * math.sqrt(0.5)))).astype(BF16)
        return carry

    lax.fori_loop(0, cells_y // 2, some, 0)


def skip_tables(skip, bias, width):
    copies = width // skip.shape[0]
    same = jnp.eye(copies, dtype=bool)[:, None, :, None]
    wide = jnp.where(same, skip[None, :, None, :], jnp.zeros((), skip.dtype))
    return wide.reshape(width, width), jnp.tile(bias, copies).reshape(1, width)


def layer_back(second, third, modes, grid, wide_skip, wide_bias, groups):
    rows, lanes = grid.shape
    depth = modes.shape[0]
    width = wide_skip.shape[0]
    return pl.pallas_call(
        functools.partial(layer_body, groups),
        grid=(lanes // width,),
        in_specs=[
            pl.BlockSpec(second.shape, lambda i: (0, 0)),
            pl.BlockSpec(third.shape, lambda i: (0, 0)),
            pl.BlockSpec((depth, width), lambda i: (0, i)),
            pl.BlockSpec((rows, width), lambda i: (0, i)),
            pl.BlockSpec((width, width), lambda i: (0, 0)),
            pl.BlockSpec((1, width), lambda i: (0, 0)),
        ],
        out_specs=pl.BlockSpec((rows, width), lambda i: (0, i)),
        out_shape=jax.ShapeDtypeStruct((rows, lanes), BF16),
        scratch_shapes=[pltpu.VMEM((groups * second.shape[0], width), F32)],
        compiler_params=pltpu.CompilerParams(vmem_limit_bytes=40 * 1024 * 1024),
        cost_estimate=pl.CostEstimate(
            flops=2 * rows * lanes * depth,
            bytes_accessed=2 * rows * (depth + 2 * lanes),
            transcendentals=rows * lanes,
        ),
        name="layer_back",
    )(second, third, modes, grid, wide_skip, wide_bias)


def swap(values, distance, size):
    return lax.ppermute(values, "py", [(i, i ^ distance) for i in range(size)])


def reduced_modes(grid, forward, size):
    lanes = grid.shape[1]
    held = forward_modes(*forward, grid, size)
    held = held.reshape(size, -1, lanes)
    distance = 1
    while distance < size:
        halves = held.reshape(held.shape[0] // 2, 2, -1, lanes)
        came = swap(halves[:, 1], distance, size)
        held = (halves[:, 0].astype(F32) + came.astype(F32)).astype(BF16)
        distance *= 2
    return held


def gathered_modes(held, size):
    distance = size // 2
    while distance >= 1:
        came = swap(held, distance, size)
        held = jnp.stack([held, came], axis=1).reshape(-1, held.shape[1], held.shape[2])
        distance //= 2
    return held.reshape(-1, held.shape[2])


def exchange_x(values):
    return lax.all_to_all(values, "px", split_axis=0, concat_axis=0, tiled=True)


def spectral_modes(grids, weights, forward, first_forward, first_back_table, size):
    rows_px = lax.axis_size("px")
    channels = weights.shape[3]
    ky_dev, kz_dev = weights.shape[1], weights.shape[2]
    lanes = grids[0].shape[1]
    x_chunk = lanes // channels
    first_modes = 0.0
    for at, grid in enumerate(grids):
        own = reduced_modes(grid, forward, size).reshape(rows_px, -1, lanes)
        lines = exchange_x(own).reshape(rows_px, ky_dev, kz_dev, 2, x_chunk, channels)
        first_modes += jnp.einsum(
            "skzpxc,sxpmq->mkzqc",
            lines,
            first_forward[:, at * x_chunk : (at + 1) * x_chunk],
            preferred_element_type=F32,
        )
    product = jnp.einsum(
        "mkzpc,mkzcr->mkzpr", first_modes.astype(BF16), weights, preferred_element_type=F32
    )
    mixed = jnp.stack(
        [
            product[..., 0, :channels] - product[..., 1, channels:],
            product[..., 0, channels:] + product[..., 1, :channels],
        ],
        axis=3,
    ).astype(BF16)
    modes = []
    for at in range(len(grids)):
        first_back = jnp.einsum(
            "mkzpc,mpsxq->skzqxc",
            mixed,
            first_back_table[:, :, :, at * x_chunk : (at + 1) * x_chunk],
            preferred_element_type=F32,
        ).astype(BF16)
        back = exchange_x(first_back.reshape(rows_px, -1, lanes))
        modes.append(gathered_modes(back.reshape(1, -1, lanes), size))
    return modes


def slot_plan(block_bricks, bricks_device, slot_total, capacity):
    owners = block_bricks[:, 0] // bricks_device
    order_index = jnp.arange(owners.shape[0], dtype=jnp.int32)
    earlier = (owners[None, :] == owners[:, None]) & (order_index[None, :] < order_index[:, None])
    ranking = jnp.sum(earlier.astype(jnp.int32), axis=1)
    slot_index = owners * capacity + ranking
    matching = slot_index[None, :] == jnp.arange(slot_total, dtype=jnp.int32)[:, None]
    present = jnp.any(matching, axis=1)
    sources = jnp.sum(jnp.where(matching, order_index[None, :], 0), axis=1)
    return (slot_index, present, sources)


def pack_slots(values, present, sources, filler):
    picked = jnp.take(values, sources, axis=0)
    masking = present.reshape((-1,) + (1,) * (values.ndim - 1))
    return jnp.where(masking, picked, jnp.asarray(filler, values.dtype))


def route_back(values):
    return lax.all_to_all(values, ("px", "py"), split_axis=0, concat_axis=0, tiled=True)


def per_device(
    point_channel_values,
    point_offsets,
    point_counts,
    block_bricks,
    spectral_weights,
    skip_weights,
    skip_bias,
):
    mesh_rows = lax.axis_size("px")
    mesh_columns = lax.axis_size("py")
    device_total = mesh_rows * mesh_columns
    capacity = max(2, 2 * point_channel_values.shape[0] // device_total)
    channels, points = point_channel_values.shape[1:]
    x_dev, y_dev = NX // mesh_rows, NY // mesh_columns
    bricks_y = y_dev // 4
    bricks_z = NZ // 16
    bricks_device = x_dev // 2 * bricks_y * bricks_z
    slot_total = device_total * capacity
    local_ids = block_bricks % bricks_device
    slot_index, present, sources = slot_plan(block_bricks, bricks_device, slot_total, capacity)
    coordinates = jnp.stack(
        [local_ids // (bricks_y * bricks_z), local_ids // bricks_z % bricks_y, local_ids % bricks_z],
        axis=-1,
    ).reshape(local_ids.shape[0], -1)
    facts = jnp.concatenate([coordinates, point_counts[:, None]], axis=1).astype(BF16)
    facts = jnp.pad(facts, ((0, 0), (0, points - facts.shape[1])))
    notes = jnp.concatenate([point_offsets, facts[:, None, :]], axis=1)
    packed_notes = pack_slots(notes, present, sources, 0)
    packed_features = pack_slots(point_channel_values, present, sources, 0)
    got_notes = route_back(packed_notes)
    got_features = route_back(packed_features)
    info = got_notes[:, 3, :13].astype(jnp.int32).reshape(-1)

    kz_dev = MODES // mesh_columns
    me_y = lax.axis_index("py")
    index = jnp.arange(2 * MODES, dtype=jnp.int32)
    group_at = jnp.bitwise_xor(index // (2 * kz_dev), me_y)
    kz = index // 2 % kz_dev + kz_dev * group_at
    angle_z = unit_angles(kz[:, None] * jnp.arange(NZ, dtype=jnp.int32)[None, :], NZ)
    third = jnp.where((index % 2 == 0)[:, None], jnp.cos(angle_z), -jnp.sin(angle_z))
    third = third / math.sqrt(NZ)
    fold = jnp.where(kz == 0, 1.0, 2.0).astype(F32)[:, None]
    third_back = (third * fold).T.astype(BF16)
    span = 2 * kz_dev
    row = jnp.arange(MODES * span, dtype=jnp.int32)[:, None]
    column = jnp.arange(y_dev * span, dtype=jnp.int32)[None, :]
    ky_at = row // span
    ky = jnp.where(ky_at < MODES // 2, ky_at, ky_at - MODES)
    angle_y = unit_angles(ky * (me_y * y_dev + column // span), NY)
    row_part, column_part = row % 2, column % 2
    sine = jnp.where(row_part == 0, jnp.sin(angle_y), -jnp.sin(angle_y))
    second = jnp.where(row_part == column_part, jnp.cos(angle_y), sine) / math.sqrt(NY)
    second = jnp.where(row % span // 2 == column % span // 2, second, 0.0).astype(BF16)
    forward = (third.astype(BF16), second)
    back = (second.T, third_back)
    first_matrix = forward_matrix(NX, wave_numbers(MODES))
    first_forward = first_matrix.reshape(mesh_rows, x_dev, 2, MODES, 2).astype(BF16)
    first_back = (
        first_matrix.transpose(2, 3, 0, 1).reshape(MODES, 2, mesh_rows, x_dev, 2).astype(BF16)
    )
    lanes = x_dev * channels
    width = math.gcd(lanes // CHUNKS, 4 * channels)
    skips = [skip_tables(skip_weights[at], skip_bias[at], width) for at in range(LAYERS)]
    got_features, forward, back, first_forward, first_back, skips = lax.optimization_barrier(
        (got_features, forward, back, first_forward, first_back, skips)
    )
    grids = encode(info, got_features, got_notes, y_dev * NZ, NZ, lanes)
    for depth_index in range(LAYERS):
        modes = spectral_modes(
            grids, spectral_weights[depth_index], forward, first_forward, first_back, mesh_columns
        )
        grids = [
            layer_back(*back, mode, grid, *skips[depth_index], mesh_columns)
            for mode, grid in zip(modes, grids)
        ]
    reply = decode(info, grids, got_notes, channels, NZ)
    returned = route_back(reply)
    return jnp.take(returned, slot_index, axis=0)


def solution(mesh):
    return jax.shard_map(
        per_device,
        mesh=mesh,
        in_specs=(
            P(("px", "py"), None, None),
            P(("px", "py"), None, None),
            P(("px", "py")),
            P(("px", "py"), None),
            P(None, None, "px", "py", None, None),
            P(),
            P(),
        ),
        out_specs=P(("px", "py"), None, None),
        check_vma=False,
    )
```

```python
import functools
import math

import jax
import jax.numpy as jnp
from jax import lax
from jax.experimental import pallas as pl
from jax.experimental.pallas import tpu as pltpu
from jax.sharding import PartitionSpec as P

MODES = 32
NX = 128
NY = 128
NZ = 128
LAYERS = 2

AMPLITUDE = 0.25
SPREAD = 4.5
DECODE_SCALE = 0.1
CHUNKS = 2
WAYS = 4
VMEM_LIMIT = 60 * 1024 * 1024
F32 = jnp.float32
BF16 = jnp.bfloat16


def wave_numbers(kept_modes):
    position = jnp.arange(kept_modes, dtype=jnp.int32)
    return jnp.where(position < kept_modes // 2, position, position - kept_modes)


def forward_matrix(length, frequency):
    places = jnp.arange(length, dtype=jnp.int32)
    products = jnp.remainder(places[:, None] * frequency[None, :], length)
    angles = 2.0 * math.pi / length * products.astype(F32)
    cosine = jnp.cos(angles) / math.sqrt(length)
    sine_part = jnp.sin(angles) / math.sqrt(length)
    from_real = jnp.stack([cosine, -sine_part], axis=-1)
    from_imag = jnp.stack([sine_part, cosine], axis=-1)
    return jnp.stack([from_real, from_imag], axis=1)


def unit_angles(products, length):
    return 2.0 * math.pi / length * jnp.remainder(products, length).astype(F32)


def block_kernel(info_ref, slot, offsets, points):
    base = slot * 13
    count = info_ref[base + 12]
    lanes = lax.broadcasted_iota(jnp.int32, (1, points), 1)
    amplitude = jnp.where(lanes < count, AMPLITUDE, 0.0).astype(F32)

    def part(dim, brick, cells, scale):
        shift = ((info_ref[base + 3 * brick + dim] - info_ref[base + dim]) * scale).astype(F32)
        center = lax.broadcasted_iota(jnp.int32, (cells, points), 0).astype(F32) + 0.5
        apart = (offsets[dim : dim + 1, :] - shift) - center
        return jnp.exp(apart * apart * (-1.0 / SPREAD))

    rows = []
    for brick in range(4):
        along_x = part(0, brick, 2, 2) * amplitude
        along_y = part(1, brick, 4, 4)
        along_z = part(2, brick, 16, 16)
        for cy in range(4):
            plane = along_z * along_y[cy : cy + 1, :]
            rows.append(
                jnp.concatenate(
                    [plane * along_x[0:1, :], plane * along_x[1:2, :]], axis=1
                ).astype(BF16)
            )
    return jnp.concatenate(rows, axis=0)


def brick_place(info_ref, slot, brick, cy, depth):
    base = slot * 13 + 3 * brick
    row = (info_ref[base + 1] * 4 + cy) * depth + info_ref[base + 2] * 16
    return (
        pl.ds(pl.multiple_of(row, 16), 16),
        pl.ds(pl.multiple_of(info_ref[base] * 128, 128), 128),
    )


def encode_body(group, depth, steps, info_ref, feature_ref, offset_ref, *refs):
    out_refs, total_ref = refs[:-1], refs[-1]
    step = pl.program_id(0)

    @pl.when(step == 0)
    def _():
        total_ref[...] = jnp.zeros_like(total_ref)

    def some(turn, carry):
        tiles = []
        for way in range(WAYS):
            member = turn * WAYS + way
            values = block_kernel(
                info_ref, step * group + member, offset_ref[member].astype(F32), offset_ref.shape[2]
            )
            feature = feature_ref[member]
            empty = jnp.zeros_like(feature)
            pair = jnp.concatenate(
                [
                    jnp.concatenate([feature, empty], axis=1),
                    jnp.concatenate([empty, feature], axis=1),
                ],
                axis=0,
            )
            tiles.append(
                lax.dot_general(values, pair, (((1,), (1,)), ((), ())), preferred_element_type=F32)
            )
        for way in range(WAYS):
            slot = step * group + turn * WAYS + way
            rounded = tiles[way].astype(BF16).astype(F32)
            places = [
                brick_place(info_ref, slot, brick, cy, depth)
                for brick in range(4)
                for cy in range(4)
            ]
            sums = [
                total_ref[place] + rounded[16 * at : 16 * at + 16, :]
                for at, place in enumerate(places)
            ]
            for place, value in zip(places, sums):
                total_ref[place] = value

        return carry

    lax.fori_loop(0, group // WAYS, some, 0)

    @pl.when(step == steps - 1)
    def _():
        for at, out_ref in enumerate(out_refs):
            width = out_ref.shape[1]
            out_ref[...] = total_ref[:, at * width : (at + 1) * width].astype(BF16)


def encode(info, features, offsets, rows, depth, lanes):
    slots, channels, points = features.shape
    group = math.gcd(slots, 32)
    steps = slots // group
    width = lanes // CHUNKS
    return pl.pallas_call(
        functools.partial(encode_body, group, depth, steps),
        grid_spec=pltpu.PrefetchScalarGridSpec(
            num_scalar_prefetch=1,
            grid=(steps,),
            in_specs=[
                pl.BlockSpec((group, channels, points), lambda i, info: (i, 0, 0)),
                pl.BlockSpec((group, offsets.shape[1], points), lambda i, info: (i, 0, 0)),
            ],
            out_specs=[pl.BlockSpec((rows, width), lambda i, info: (0, 0))] * CHUNKS,
            scratch_shapes=[pltpu.VMEM((rows, lanes), F32)],
        ),
        out_shape=[jax.ShapeDtypeStruct((rows, width), BF16)] * CHUNKS,
        compiler_params=pltpu.CompilerParams(vmem_limit_bytes=VMEM_LIMIT),
        name="encode",
    )(info, features, offsets)


def decode_body(group, depth, info_ref, *refs):
    grid_refs, offset_ref, out_ref, held_ref = refs[:CHUNKS], refs[-3], refs[-2], refs[-1]
    step = pl.program_id(0)
    channels, points = out_ref.shape[1:]

    @pl.when(step == 0)
    def _():
        for at, grid_ref in enumerate(grid_refs):
            width = grid_ref.shape[1]
            held_ref[:, at * width : (at + 1) * width] = grid_ref[...]

    def some(turn, carry):
        results = []
        for way in range(WAYS):
            member = turn * WAYS + way
            slot = step * group + member
            values = block_kernel(info_ref, slot, offset_ref[member].astype(F32), points)
            cells = jnp.concatenate(
                [
                    held_ref[brick_place(info_ref, slot, brick, cy, depth)]
                    for brick in range(4)
                    for cy in range(4)
                ],
                axis=0,
            )
            both = lax.dot_general(
                cells, values, (((0,), (0,)), ((), ())), preferred_element_type=F32
            )
            summed = both[:channels, :points] + both[channels:, points:]
            results.append((DECODE_SCALE * summed).astype(BF16))
        for way in range(WAYS):
            out_ref[turn * WAYS + way] = results[way]
        return carry

    lax.fori_loop(0, group // WAYS, some, 0)


def decode(info, grids, offsets, channels, depth):
    slots, rows3, points = offsets.shape
    group = math.gcd(slots, 32)
    rows, width = grids[0].shape
    return pl.pallas_call(
        functools.partial(decode_body, group, depth),
        grid_spec=pltpu.PrefetchScalarGridSpec(
            num_scalar_prefetch=1,
            grid=(slots // group,),
            in_specs=[pl.BlockSpec((rows, width), lambda i, info: (0, 0))] * CHUNKS
            + [pl.BlockSpec((group, rows3, points), lambda i, info: (i, 0, 0))],
            out_specs=pl.BlockSpec((group, channels, points), lambda i, info: (i, 0, 0)),
            scratch_shapes=[pltpu.VMEM((rows, width * CHUNKS), BF16)],
        ),
        out_shape=jax.ShapeDtypeStruct((slots, channels, points), BF16),
        compiler_params=pltpu.CompilerParams(vmem_limit_bytes=VMEM_LIMIT),
        cost_estimate=pl.CostEstimate(
            flops=4 * slots * channels * points * 512,
            bytes_accessed=2 * rows * width * CHUNKS,
            transcendentals=slots * points * 128,
        ),
        name="decode",
    )(info, *grids, offsets)


def forward_body(groups, third_ref, second_ref, grid_ref, out_ref, held_ref):
    depth = third_ref.shape[1]
    span = third_ref.shape[0] // groups
    cells_y = grid_ref.shape[0] // depth
    count_in, count_out = second_ref.shape[1], second_ref.shape[0]

    def some(turn, carry):
        for way in range(WAYS):
            y = turn * WAYS + way
            line = grid_ref[pl.ds(pl.multiple_of(y * depth, depth), depth), :]
            modes = jnp.dot(third_ref[...], line, preferred_element_type=F32)
            for at in range(groups):
                row = pl.multiple_of(at * count_in + y * span, span)
                held_ref[pl.ds(row, span), :] = modes[at * span : (at + 1) * span, :]
        return carry

    lax.fori_loop(0, cells_y // WAYS, some, 0)
    for at in range(groups):
        third = held_ref[at * count_in : (at + 1) * count_in, :].astype(BF16)
        out_ref[at * count_out : (at + 1) * count_out, :] = jnp.dot(
            second_ref[...], third, preferred_element_type=F32
        ).astype(BF16)


def forward_modes(third, second, grid, groups):
    rows, lanes = grid.shape
    count_out, count_in = second.shape
    width = math.gcd(lanes, 256)
    return pl.pallas_call(
        functools.partial(forward_body, groups),
        grid=(lanes // width,),
        in_specs=[
            pl.BlockSpec(third.shape, lambda i: (0, 0)),
            pl.BlockSpec(second.shape, lambda i: (0, 0)),
            pl.BlockSpec((rows, width), lambda i: (0, i)),
        ],
        out_specs=pl.BlockSpec((groups * count_out, width), lambda i: (0, i)),
        out_shape=jax.ShapeDtypeStruct((groups * count_out, lanes), BF16),
        scratch_shapes=[pltpu.VMEM((groups * count_in, width), F32)],
        compiler_params=pltpu.CompilerParams(vmem_limit_bytes=40 * 1024 * 1024),
        cost_estimate=pl.CostEstimate(
            flops=8 * groups * lanes * count_out * count_in,
            bytes_accessed=2 * lanes * (rows + groups * count_out),
            transcendentals=0,
        ),
        name="forward_modes",
    )(third, second, grid)


def layer_body(groups, second_ref, third_ref, modes_ref, grid_ref, skip_ref, bias_ref, out_ref, held_ref):
    depth = third_ref.shape[0]
    span = third_ref.shape[1] // groups
    cells_y = grid_ref.shape[0] // depth
    count_out, count_in = second_ref.shape
    for at in range(groups):
        held_ref[at * count_out : (at + 1) * count_out, :] = jnp.dot(
            second_ref[...],
            modes_ref[at * count_in : (at + 1) * count_in, :],
            preferred_element_type=F32,
        )

    def some(turn, carry):
        for way in range(2):
            y = turn * 2 + way
            pieces = []
            for at in range(groups):
                row = pl.multiple_of(at * count_out + y * span, span)
                pieces.append(held_ref[pl.ds(row, span), :])
            line = jnp.concatenate(pieces, axis=0).astype(BF16)
            place = pl.ds(pl.multiple_of(y * depth, depth), depth)
            spectral = jnp.dot(third_ref[...], line, preferred_element_type=F32)
            skipped = jnp.dot(grid_ref[place, :], skip_ref[...], preferred_element_type=F32)
            value = spectral + skipped + bias_ref[...]
            out_ref[place, :] = (0.5 * value * (1.0 + lax.erf(value * math.sqrt(0.5)))).astype(BF16)
        return carry

    lax.fori_loop(0, cells_y // 2, some, 0)


def skip_tables(skip, bias, width):
    copies = width // skip.shape[0]
    same = jnp.eye(copies, dtype=bool)[:, None, :, None]
    wide = jnp.where(same, skip[None, :, None, :], jnp.zeros((), skip.dtype))
    return wide.reshape(width, width), jnp.tile(bias, copies).reshape(1, width)


def layer_back(second, third, modes, grid, wide_skip, wide_bias, groups):
    rows, lanes = grid.shape
    depth = modes.shape[0]
    width = wide_skip.shape[0]
    return pl.pallas_call(
        functools.partial(layer_body, groups),
        grid=(lanes // width,),
        in_specs=[
            pl.BlockSpec(second.shape, lambda i: (0, 0)),
            pl.BlockSpec(third.shape, lambda i: (0, 0)),
            pl.BlockSpec((depth, width), lambda i: (0, i)),
            pl.BlockSpec((rows, width), lambda i: (0, i)),
            pl.BlockSpec((width, width), lambda i: (0, 0)),
            pl.BlockSpec((1, width), lambda i: (0, 0)),
        ],
        out_specs=pl.BlockSpec((rows, width), lambda i: (0, i)),
        out_shape=jax.ShapeDtypeStruct((rows, lanes), BF16),
        scratch_shapes=[pltpu.VMEM((groups * second.shape[0], width), F32)],
        compiler_params=pltpu.CompilerParams(vmem_limit_bytes=40 * 1024 * 1024),
        cost_estimate=pl.CostEstimate(
            flops=2 * rows * lanes * depth,
            bytes_accessed=2 * rows * (depth + 2 * lanes),
            transcendentals=rows * lanes,
        ),
        name="layer_back",
    )(second, third, modes, grid, wide_skip, wide_bias)


def swap(values, distance, size):
    return lax.ppermute(values, "py", [(i, i ^ distance) for i in range(size)])


def reduced_modes(grid, forward, size):
    lanes = grid.shape[1]
    held = forward_modes(*forward, grid, size)
    held = held.reshape(size, -1, lanes)
    distance = 1
    while distance < size:
        halves = held.reshape(held.shape[0] // 2, 2, -1, lanes)
        came = swap(halves[:, 1], distance, size)
        held = (halves[:, 0].astype(F32) + came.astype(F32)).astype(BF16)
        distance *= 2
    return held


def gathered_modes(held, size):
    distance = size // 2
    while distance >= 1:
        came = swap(held, distance, size)
        held = jnp.stack([held, came], axis=1).reshape(-1, held.shape[1], held.shape[2])
        distance //= 2
    return held.reshape(-1, held.shape[2])


def exchange_x(values):
    return lax.all_to_all(values, "px", split_axis=0, concat_axis=0, tiled=True)


def spectral_modes(grids, weights, forward, first_forward, first_back_table, size):
    rows_px = lax.axis_size("px")
    channels = weights.shape[3]
    ky_dev, kz_dev = weights.shape[1], weights.shape[2]
    lanes = grids[0].shape[1]
    x_chunk = lanes // channels
    first_modes = 0.0
    for at, grid in enumerate(grids):
        own = reduced_modes(grid, forward, size).reshape(rows_px, -1, lanes)
        lines = exchange_x(own).reshape(rows_px, ky_dev, kz_dev, 2, x_chunk, channels)
        first_modes += jnp.einsum(
            "skzpxc,sxpmq->mkzqc",
            lines,
            first_forward[:, at * x_chunk : (at + 1) * x_chunk],
            preferred_element_type=F32,
        )
    product = jnp.einsum(
        "mkzpc,mkzcr->mkzpr", first_modes.astype(BF16), weights, preferred_element_type=F32
    )
    mixed = jnp.stack(
        [
            product[..., 0, :channels] - product[..., 1, channels:],
            product[..., 0, channels:] + product[..., 1, :channels],
        ],
        axis=3,
    ).astype(BF16)
    modes = []
    for at in range(len(grids)):
        first_back = jnp.einsum(
            "mkzpc,mpsxq->skzqxc",
            mixed,
            first_back_table[:, :, :, at * x_chunk : (at + 1) * x_chunk],
            preferred_element_type=F32,
        ).astype(BF16)
        back = exchange_x(first_back.reshape(rows_px, -1, lanes))
        modes.append(gathered_modes(back.reshape(1, -1, lanes), size))
    return modes


def slot_plan(block_bricks, bricks_device, slot_total, capacity):
    owners = block_bricks[:, 0] // bricks_device
    order_index = jnp.arange(owners.shape[0], dtype=jnp.int32)
    earlier = (owners[None, :] == owners[:, None]) & (order_index[None, :] < order_index[:, None])
    ranking = jnp.sum(earlier.astype(jnp.int32), axis=1)
    slot_index = owners * capacity + ranking
    matching = slot_index[None, :] == jnp.arange(slot_total, dtype=jnp.int32)[:, None]
    present = jnp.any(matching, axis=1)
    sources = jnp.sum(jnp.where(matching, order_index[None, :], 0), axis=1)
    return (slot_index, present, sources)


def pack_slots(values, present, sources, filler):
    picked = jnp.take(values, sources, axis=0, mode="clip")
    masking = present.reshape((-1,) + (1,) * (values.ndim - 1))
    return jnp.where(masking, picked, jnp.asarray(filler, values.dtype))


def route_back(values):
    return lax.all_to_all(values, ("px", "py"), split_axis=0, concat_axis=0, tiled=True)


def per_device(
    point_channel_values,
    point_offsets,
    point_counts,
    block_bricks,
    spectral_weights,
    skip_weights,
    skip_bias,
):
    mesh_rows = lax.axis_size("px")
    mesh_columns = lax.axis_size("py")
    device_total = mesh_rows * mesh_columns
    capacity = max(2, 2 * point_channel_values.shape[0] // device_total)
    channels, points = point_channel_values.shape[1:]
    x_dev, y_dev = NX // mesh_rows, NY // mesh_columns
    bricks_y = y_dev // 4
    bricks_z = NZ // 16
    bricks_device = x_dev // 2 * bricks_y * bricks_z
    slot_total = device_total * capacity
    local_ids = block_bricks % bricks_device
    slot_index, present, sources = slot_plan(block_bricks, bricks_device, slot_total, capacity)
    coordinates = jnp.stack(
        [local_ids // (bricks_y * bricks_z), local_ids // bricks_z % bricks_y, local_ids % bricks_z],
        axis=-1,
    ).reshape(local_ids.shape[0], -1)
    facts = jnp.concatenate([coordinates, point_counts[:, None]], axis=1).astype(BF16)
    facts = jnp.pad(facts, ((0, 0), (0, points - facts.shape[1])))
    notes = jnp.concatenate([point_offsets, facts[:, None, :]], axis=1)
    packed_notes = pack_slots(notes, present, sources, 0)
    packed_features = pack_slots(point_channel_values, present, sources, 0)
    got_notes = route_back(packed_notes)
    got_features = route_back(packed_features)
    info = got_notes[:, 3, :13].astype(jnp.int32).reshape(-1)

    kz_dev = MODES // mesh_columns
    me_y = lax.axis_index("py")
    index = jnp.arange(2 * MODES, dtype=jnp.int32)
    group_at = jnp.bitwise_xor(index // (2 * kz_dev), me_y)
    kz = index // 2 % kz_dev + kz_dev * group_at
    angle_z = unit_angles(kz[:, None] * jnp.arange(NZ, dtype=jnp.int32)[None, :], NZ)
    third = jnp.where((index % 2 == 0)[:, None], jnp.cos(angle_z), -jnp.sin(angle_z))
    third = third / math.sqrt(NZ)
    fold = jnp.where(kz == 0, 1.0, 2.0).astype(F32)[:, None]
    third_back = (third * fold).T.astype(BF16)
    span = 2 * kz_dev
    row = jnp.arange(MODES * span, dtype=jnp.int32)[:, None]
    column = jnp.arange(y_dev * span, dtype=jnp.int32)[None, :]
    ky_at = row // span
    ky = jnp.where(ky_at < MODES // 2, ky_at, ky_at - MODES)
    angle_y = unit_angles(ky * (me_y * y_dev + column // span), NY)
    row_part, column_part = row % 2, column % 2
    sine = jnp.where(row_part == 0, jnp.sin(angle_y), -jnp.sin(angle_y))
    second = jnp.where(row_part == column_part, jnp.cos(angle_y), sine) / math.sqrt(NY)
    second = jnp.where(row % span // 2 == column % span // 2, second, 0.0).astype(BF16)
    forward = (third.astype(BF16), second)
    back = (second.T, third_back)
    first_matrix = forward_matrix(NX, wave_numbers(MODES))
    first_forward = first_matrix.reshape(mesh_rows, x_dev, 2, MODES, 2).astype(BF16)
    first_back = (
        first_matrix.transpose(2, 3, 0, 1).reshape(MODES, 2, mesh_rows, x_dev, 2).astype(BF16)
    )
    lanes = x_dev * channels
    width = math.gcd(lanes // CHUNKS, 4 * channels)
    skips = [skip_tables(skip_weights[at], skip_bias[at], width) for at in range(LAYERS)]
    got_features, forward, back, first_forward, first_back, skips = lax.optimization_barrier(
        (got_features, forward, back, first_forward, first_back, skips)
    )
    grids = encode(info, got_features, got_notes, y_dev * NZ, NZ, lanes)
    for depth_index in range(LAYERS):
        modes = spectral_modes(
            grids, spectral_weights[depth_index], forward, first_forward, first_back, mesh_columns
        )
        grids = [
            layer_back(*back, mode, grid, *skips[depth_index], mesh_columns)
            for mode, grid in zip(modes, grids)
        ]
    half = capacity // 2
    ranks = slot_index % capacity
    at_half = slot_index // capacity * half + ranks % half
    infos = info.reshape(device_total, 2, -1)
    halved_notes = got_notes.reshape((device_total, 2, half) + got_notes.shape[1:])
    picked = []
    for side in range(2):
        side_notes = halved_notes[:, side].reshape((-1,) + got_notes.shape[1:])
        reply = decode(infos[:, side].reshape(-1), grids, side_notes, channels, NZ)
        picked.append(jnp.take(route_back(reply), at_half, axis=0, mode="clip"))
    return jnp.where((ranks < half)[:, None, None], picked[0], picked[1])


def solution(mesh):
    return jax.shard_map(
        per_device,
        mesh=mesh,
        in_specs=(
            P(("px", "py"), None, None),
            P(("px", "py"), None, None),
            P(("px", "py")),
            P(("px", "py"), None),
            P(None, None, "px", "py", None, None),
            P(),
            P(),
        ),
        out_specs=P(("px", "py"), None, None),
        check_vma=False,
    )
```
